128 devices in a mesh: row: 8 (over x, y_hi), col: 16 (over z, y_lo, core).
Axes of the slice: x: 4, y: 4 (y_hi: 2, y_lo: 2; y = y_hi * 2 + y_lo), z: 4, core: 2. Of those that a mesh axis runs over, the one named last changes fastest.
Arguments:
- normal_slab: float32 [8192, 16384], P('row', 'col'), may hold values from -6 to 6
- left_design: float32 [3, 1024, 8192], P(None, 'col', 'row'), may hold values from -1.2 to 1.2
- right_design: float32 [3, 1024, 16384], P(None, 'row', 'col'), may hold values from -1.2 to 1.2
- estimate: float32 [16384], P('col'), may hold values from -0.25 to 0.25
- observed: float32 [3, 1024], P(None, 'row'), may hold values from -6 to 6
- arc_id: int32 [3, 1024], P(None, 'row'), may hold values from 0 to 63
- arc_bias: float32 [64], replicated, may hold values from -5 to 5
Outputs:
- updated_slab: float32 [8192, 16384], P('row', 'col')
The draws below stay inside these ranges and needn't reach their ends.
All inputs are finite; a program needn't handle non-finite values.
Results may differ from the reference program's by a relative error of at most 0.0001.
Values sent between devices are 32-bit elements; how exact they have to be, the bound alone decides.
A program may use at most 128 MiB of HBM per device.

```python
import jax
import jax.numpy as jnp
from jax import lax

R = 8192
C = 16384
GROUP_OBS = 1024
GROUPS = 3
ARCS = 64


def set_ends(entries, own_key, low, top_value):
    dims = entries.shape
    index_at = [jax.random.randint(jax.random.fold_in(own_key, axis), (), 0, dims[axis]) for axis in range(len(dims))]
    entries = entries.at[tuple(index_at)].set(low)
    longest = dims.index(max(dims))
    index_at[longest] = (index_at[longest] + 1) % dims[longest]
    return entries.at[tuple(index_at)].set(top_value)


def level_of(own_key, dims, split, least, largest):
    gain = 1.0
    for dim, blocks in split:
        draws = jax.random.uniform(jax.random.fold_in(jax.random.fold_in(own_key, 6), dim), (blocks,), jnp.float32, least / len(split), largest / len(split))
        gain = gain * jnp.repeat(jnp.exp(draws), dims[dim] // blocks).reshape((-1,) + (1,) * (len(dims) - 1 - dim))
    return gain


def scatter_about(own_key, extent, scale, limit, cuts=(), held_as=jnp.bfloat16):
    entries = scale * jax.random.normal(own_key, extent, jnp.float32)
    if cuts:
        entries = entries * level_of(own_key, extent, cuts, -0.22, 0.18)
    return jnp.clip(entries, -limit, limit).astype(held_as)


def setup_inputs(seed: int = 0) -> dict:
    keys = jax.random.split(jax.random.key(seed), 8)
    normal_slab = scatter_about(keys[0], (R, C), 1.0, 6.0, ((0, 8), (1, 16)), jnp.float32)
    left_design = scatter_about(keys[1], (GROUPS, GROUP_OBS, R), 0.2, 1.2, ((1, 16), (2, 8)), jnp.float32)
    right_design = scatter_about(keys[2], (GROUPS, GROUP_OBS, C), 0.2, 1.2, ((1, 8), (2, 16)), jnp.float32)
    estimate = scatter_about(keys[3], (C,), (C // 25) ** -0.5, 0.25, ((0, 16),), jnp.float32)
    observed = scatter_about(keys[4], (GROUPS, GROUP_OBS), 1.0, 6.0, ((1, 8),), jnp.float32)
    arc_id = set_ends(jax.random.randint(keys[5], (GROUPS, GROUP_OBS), 0, ARCS), jax.random.fold_in(keys[5], 1), 0, ARCS - 1).astype(jnp.int32)
    arc_bias = scatter_about(keys[6], (ARCS,), 1.0, 5.0, (), jnp.float32)
    return dict(normal_slab=normal_slab, left_design=left_design, right_design=right_design, estimate=estimate, observed=observed, arc_id=arc_id, arc_bias=arc_bias)


def reference(normal_slab, left_design, right_design, estimate, observed, arc_id, arc_bias):
    highest = lax.Precision.HIGHEST
    running = normal_slab
    for number in range(GROUPS):
        predicted = jnp.dot(right_design[number], estimate, precision=highest)
        residual = observed[number] - predicted - arc_bias[arc_id[number]]
        weights = 1.0 / (1.0 + residual * residual)
        scaled = left_design[number] * weights[:, None]
        running = running + jnp.dot(scaled.T, right_design[number], precision=highest)
    return running
```

```python
import functools

import jax
import jax.numpy as jnp
from jax import lax
from jax.experimental import pallas as pl
from jax.experimental.pallas import tpu as pltpu
from jax.sharding import PartitionSpec as P

MESH = pl.DeviceIdType.MESH
F32, BF16 = jnp.float32, jnp.bfloat16
NX, NZ = 4, 4
TILE = 256


def kernel(est, obs, arc, bias, slab, left, right, out, rbuf, lbuf, lt, psend, pbuf, wbuf,
           rs, rr, ls, lr, ps, pr, ws, wr, cs):
    groups, n_obs, width = right.shape
    half, quarter = n_obs // 2, n_obs // 4
    row, col = lax.axis_index("row"), lax.axis_index("col")
    x, h = row // 2, row % 2
    z, l, k = col // 4, (col // 2) % 2, col % 2

    def unit_r(dx, flip=0):
        return ((x + dx) % NX) * 2 + (h + flip) % 2

    def unit_l(dz, flip=0):
        return ((z + dz) % NZ) * 2 + (l + flip) % 2

    def to_row(r):
        return (r, col)

    def to_col(c):
        return (row, c)

    x_up, x_down, y_far = to_row(unit_r(1)), to_row(unit_r(-1)), to_row(unit_r(0, 1))
    z_up, z_down = to_col(unit_l(1) * 2 + k), to_col(unit_l(-1) * 2 + k)
    y_near, sibling = to_col(unit_l(0, 1) * 2 + k), to_col((col // 2) * 2 + (1 - k))

    barrier = pltpu.get_barrier_semaphore()
    for d in range(1, 16):
        pl.semaphore_signal(barrier, inc=1, device_id=to_col((col + d) % 16), device_id_type=MESH)
    for d in range(1, 8):
        pl.semaphore_signal(barrier, inc=1, device_id=to_row((row + d) % 8), device_id_type=MESH)
    pl.semaphore_wait(barrier, 22)

    sends = []

    def remote(src, dst, s, r, target):
        return pltpu.make_async_remote_copy(
            src_ref=src, dst_ref=dst, send_sem=s, recv_sem=r, device_id=target, device_id_type=MESH
        )

    A, B = pl.ds(0, half), pl.ds(half, half)

    def r_copy(slot, unit, part, target, src=None):
        dst = rbuf.at[unit, :, part, :]
        return remote(dst if src is None else src.at[:, part, :], dst, rs.at[slot], rr.at[slot], target)

    def r_send(slot, unit, part, target, src=None):
        c = r_copy(slot, unit, part, target, src)
        c.start()
        sends.append(c)

    def r_wait(slot, unit, part):
        r_copy(slot, unit, part, y_far).wait_recv()

    def l_rows(part, core):
        if part == "a":
            return pl.ds(core * half, quarter)
        if part == "b":
            return pl.ds(core * half + quarter, quarter)
        return pl.ds(core * half, half)

    def l_copy(slot, unit, part, target, src=None, core=None):
        dst = lbuf.at[unit, :, l_rows(part, k if core is None else core), :]
        if src is not None:
            src = src.at[:, l_rows(part, 0), :]
        return remote(dst if src is None else src, dst, ls.at[slot], lr.at[slot], target)

    def l_send(slot, unit, part, target, src=None):
        c = l_copy(slot, unit, part, target, src)
        c.start()
        sends.append(c)

    def l_wait(slot, unit, part, core=None):
        l_copy(slot, unit, part, sibling, core=core).wait_recv()

    own_r, own_l = row, col // 2
    l_send(0, own_l, "", y_near, left)
    l_send(1, own_l, "a", z_up, left)
    l_send(4, own_l, "b", z_down, left)
    l_send(2, own_l, "b", z_up, left)
    l_send(3, own_l, "a", z_down, left)
    r_send(0, own_r, A, x_up, right)
    r_send(3, own_r, B, x_down, right)
    r_send(4, own_r, A, y_far, right)
    r_send(1, own_r, B, x_up, right)
    r_send(2, own_r, A, x_down, right)
    r_send(5, own_r, B, y_far, right)
    l_send(13, own_l, "", sibling, left)
    r_here = pltpu.make_async_copy(right, rbuf.at[own_r], cs.at[0])
    l_here = pltpu.make_async_copy(left, lbuf.at[own_l, :, l_rows("", k), :], cs.at[1])
    s_here = pltpu.make_async_copy(slab, out, cs.at[2])
    r_here.start()
    l_here.start()
    s_here.start()

    r_here.wait()
    e = jnp.broadcast_to(est[...], (8, width))
    psend[...] = jnp.zeros_like(psend)
    for g in range(groups):
        p = lax.dot_general(
            e, rbuf[own_r, g], (((1,), (1,)), ((), ())),
            precision=lax.Precision.HIGHEST, preferred_element_type=F32,
        )
        psend[g : g + 1, :] = p[0:1, :]
    for d in range(1, 16):
        c = remote(psend, pbuf.at[col], ps.at[d], pr.at[d], to_col((col + d) % 16))
        c.start()
        sends.append(c)
    offset = jnp.zeros((groups, n_obs), F32)
    ids = arc[...]
    for a in range(bias.shape[0]):
        offset = jnp.where(ids == a, bias[a], offset)
    pbuf[col] = psend[...]
    for d in range(1, 16):
        remote(psend, pbuf.at[(col + 16 - d) % 16], ps.at[d], pr.at[d], sibling).wait_recv()
    total = pbuf[0]
    for c in range(1, 16):
        total = total + pbuf[c]
    residual = obs[...] - total[:groups] - offset
    wbuf[row] = jnp.zeros_like(wbuf[0])
    wbuf[row, 0:groups, :] = 1.0 / (1.0 + residual * residual)
    for d in range(1, 8):
        c = remote(wbuf.at[row], wbuf.at[row], ws.at[d], wr.at[d], to_row((row + d) % 8))
        c.start()
        sends.append(c)

    def prepare(unit):
        def body(i, carry):
            cols = pl.ds(pl.multiple_of(i * TILE, TILE), TILE)
            for g in range(groups):
                t = lbuf[unit, g, :, cols].T * wbuf[unit, g : g + 1, :]
                hi = t.astype(BF16)
                lo = (t - hi.astype(F32)).astype(BF16)
                lt[unit, cols, g * n_obs : (g + 1) * n_obs] = hi
                lt[unit, cols, (groups + g) * n_obs : (groups + g + 1) * n_obs] = lo
            return carry

        lax.fori_loop(0, width // TILE, body, 0)

    depth = groups * n_obs

    def multiply(unit):
        def body(i, carry):
            cols = pl.ds(pl.multiple_of(i * TILE, TILE), TILE)
            t = rbuf[unit, :, :, cols].reshape(depth, TILE)
            hi = t.astype(BF16)
            lo = (t - hi.astype(F32)).astype(BF16)
            both = jnp.concatenate([hi, hi], axis=0)
            out[:, cols] += jnp.dot(lt[unit], both, preferred_element_type=F32) + jnp.dot(
                lt[unit, :, 0:depth], lo, preferred_element_type=F32
            )
            return carry

        lax.fori_loop(0, width // TILE, body, 0)

    l_wait(1, unit_l(-1), "a")
    l_send(5, unit_l(-1), "a", z_up)
    l_wait(4, unit_l(1), "b")
    l_send(6, unit_l(1), "b", z_down)
    l_wait(0, unit_l(0, 1), "")
    l_send(7, unit_l(0, 1), "a", z_up)
    l_send(10, unit_l(0, 1), "b", z_down)
    l_send(8, unit_l(0, 1), "b", z_up)
    l_send(9, unit_l(0, 1), "a", z_down)
    l_send(14, unit_l(0, 1), "", sibling)
    l_wait(2, unit_l(-1), "b")
    l_send(15, unit_l(-1), "", sibling)
    l_wait(3, unit_l(1), "a")
    l_send(16, unit_l(1), "", sibling)
    for d in range(1, 8):
        u = (row + 8 - d) % 8
        remote(wbuf.at[row], wbuf.at[u], ws.at[d], wr.at[d], y_far).wait_recv()
    l_here.wait()
    l_wait(13, own_l, "", 1 - k)
    prepare(own_l)
    r_wait(0, unit_r(-1), A)
    r_send(6, unit_r(-1), A, x_up)
    r_send(8, unit_r(-1), A, y_far)
    r_wait(3, unit_r(1), B)
    r_send(7, unit_r(1), B, x_down)
    r_send(9, unit_r(1), B, y_far)
    l_wait(5, unit_l(2), "a")
    l_wait(6, unit_l(2), "b")
    l_send(17, unit_l(2), "", sibling)
    r_wait(4, unit_r(0, 1), A)
    r_send(10, unit_r(0, 1), A, x_down)
    r_wait(5, unit_r(0, 1), B)
    r_send(11, unit_r(0, 1), B, x_up)
    l_wait(14, unit_l(0, 1), "", 1 - k)
    prepare(unit_l(0, 1))
    l_wait(15, unit_l(-1), "", 1 - k)
    prepare(unit_l(-1))
    l_wait(7, unit_l(-1, 1), "a")
    l_send(11, unit_l(-1, 1), "a", z_up)
    l_wait(10, unit_l(1, 1), "b")
    l_send(12, unit_l(1, 1), "b", z_down)
    l_wait(16, unit_l(1), "", 1 - k)
    prepare(unit_l(1))
    l_wait(8, unit_l(-1, 1), "b")
    l_send(18, unit_l(-1, 1), "", sibling)
    l_wait(9, unit_l(1, 1), "a")
    l_send(19, unit_l(1, 1), "", sibling)
    l_wait(17, unit_l(2), "", 1 - k)
    prepare(unit_l(2))
    l_wait(18, unit_l(-1, 1), "", 1 - k)
    prepare(unit_l(-1, 1))
    l_wait(19, unit_l(1, 1), "", 1 - k)
    prepare(unit_l(1, 1))
    r_wait(1, unit_r(-1), B)
    r_wait(2, unit_r(1), A)
    l_wait(11, unit_l(2, 1), "a")
    l_wait(12, unit_l(2, 1), "b")
    l_send(20, unit_l(2, 1), "", sibling)
    r_wait(8, unit_r(-1, 1), A)
    r_send(12, unit_r(-1, 1), A, x_up)
    r_wait(9, unit_r(1, 1), B)
    r_send(13, unit_r(1, 1), B, x_down)
    l_wait(20, unit_l(2, 1), "", 1 - k)
    prepare(unit_l(2, 1))
    s_here.wait()
    multiply(own_r)
    multiply(unit_r(-1))
    multiply(unit_r(1))
    multiply(unit_r(0, 1))
    r_wait(6, unit_r(2), A)
    r_wait(7, unit_r(2), B)
    multiply(unit_r(2))
    r_wait(10, unit_r(1, 1), A)
    multiply(unit_r(1, 1))
    r_wait(11, unit_r(-1, 1), B)
    multiply(unit_r(-1, 1))
    r_wait(12, unit_r(2, 1), A)
    r_wait(13, unit_r(2, 1), B)
    multiply(unit_r(2, 1))
    for c in sends:
        c.wait_send()


def local(normal_slab, left_design, right_design, estimate, observed, arc_id, arc_bias):
    groups, n_obs, width = right_design.shape
    rows = left_design.shape[2]
    vmem, smem, anyspace = (
        pl.BlockSpec(memory_space=m) for m in (pltpu.VMEM, pltpu.SMEM, pl.ANY)
    )
    dma = pltpu.SemaphoreType.DMA
    return pl.pallas_call(
        kernel,
        name="gather_and_update",
        out_shape=jax.ShapeDtypeStruct(normal_slab.shape, F32),
        in_specs=[vmem, vmem, vmem, smem, anyspace, anyspace, anyspace],
        out_specs=vmem,
        scratch_shapes=[
            pltpu.VMEM((8, groups, n_obs, width), F32),
            pltpu.VMEM((8, groups, n_obs, rows), F32),
            pltpu.VMEM((8, rows, 2 * groups * n_obs), BF16),
            pltpu.VMEM((8, n_obs), F32),
            pltpu.VMEM((16, 8, n_obs), F32),
            pltpu.VMEM((8, 8, n_obs), F32),
            dma((14,)), dma((14,)), dma((21,)), dma((21,)),
            dma((16,)), dma((16,)), dma((8,)), dma((8,)), dma((3,)),
        ],
        compiler_params=pltpu.CompilerParams(
            collective_id=0, has_side_effects=True, vmem_limit_bytes=60 * 1024 * 1024
        ),
    )(estimate[None, :], observed, arc_id, arc_bias, normal_slab, left_design, right_design)


def solution(mesh):
    in_specs = (
        P("row", "col"),
        P(None, "col", "row"),
        P(None, "row", "col"),
        P("col"),
        P(None, "row"),
        P(None, "row"),
        P(),
    )
    return jax.shard_map(local, mesh=mesh, in_specs=in_specs, out_specs=P("row", "col"), check_vma=False)
```

```python
import functools

import jax
import jax.numpy as jnp
from jax import lax
from jax.experimental import pallas as pl
from jax.experimental.pallas import tpu as pltpu
from jax.sharding import PartitionSpec as P

MESH = pl.DeviceIdType.MESH
F32, BF16 = jnp.float32, jnp.bfloat16
NX, NZ = 4, 4
PIECES = 4
ALONG_X = (3,)
A, B = 0, 1
TILE = 256


def kernel(est_in, obs_in, arc_in, bias_in, slab, left, right, out, rbuf, lbuf, lt, psend, pbuf, wbuf,
           est, obs, arc, bias, rs, rr, ls, lr, ps, pr, ws, wr, cs):
    groups, n_obs, width = right.shape
    half, quarter = n_obs // 2, n_obs // 4
    row, col = lax.axis_index("row"), lax.axis_index("col")
    x, h = row // 2, row % 2
    z, l, k = col // 4, (col // 2) % 2, col % 2

    def unit_r(dx, flip=0):
        return ((x + dx) % NX) * 2 + (h + flip) % 2

    def unit_l(dz, flip=0):
        return ((z + dz) % NZ) * 2 + (l + flip) % 2

    def to_row(r):
        return (r, col)

    def to_col(c):
        return (row, c)

    x_up, x_down, y_far = to_row(unit_r(1)), to_row(unit_r(-1)), to_row(unit_r(0, 1))
    z_up, z_down = to_col(unit_l(1) * 2 + k), to_col(unit_l(-1) * 2 + k)
    y_near, sibling = to_col(unit_l(0, 1) * 2 + k), to_col((col // 2) * 2 + (1 - k))

    r_here = pltpu.make_async_copy(right, rbuf.at[row], cs.at[0])
    l_here = pltpu.make_async_copy(left, lbuf.at[col // 2, :, pl.ds(k * half, half), :], cs.at[1])
    s_here = pltpu.make_async_copy(slab, out, cs.at[2])
    small = [
        pltpu.make_async_copy(src, dst, cs.at[3 + i])
        for i, (src, dst) in enumerate([(est_in, est), (obs_in, obs), (arc_in, arc), (bias_in, bias)])
    ]
    for c in [r_here, *small, l_here, s_here]:
        c.start()

    barrier = pltpu.get_barrier_semaphore()
    for d in range(1, 16):
        pl.semaphore_signal(barrier, inc=1, device_id=to_col((col + d) % 16), device_id_type=MESH)
    for d in range(1, 8):
        pl.semaphore_signal(barrier, inc=1, device_id=to_row((row + d) % 8), device_id_type=MESH)
    pl.semaphore_wait(barrier, 22)

    sends = []

    def remote(src, dst, s, r, target):
        return pltpu.make_async_remote_copy(
            src_ref=src, dst_ref=dst, send_sem=s, recv_sem=r, device_id=target, device_id_type=MESH
        )

    def r_copy(slot, unit, part, i, target, src=None):
        rows, cols = pl.ds(part * half, half), pl.ds(i * TILE, TILE)
        dst = rbuf.at[unit, :, rows, cols]
        s = slot * PIECES + i
        return remote(dst if src is None else src.at[:, rows, cols], dst, rs.at[s], rr.at[s], target)

    def r_send(slot, unit, part, i, target, src=None):
        c = r_copy(slot, unit, part, i, target, src)
        c.start()
        sends.append(c)

    def r_wait(slot, unit, part, i):
        r_copy(slot, unit, part, i, y_far).wait_recv()

    def r_all(slot, unit, part):
        for i in range(PIECES):
            r_wait(slot, unit, part, i)

    def l_rows(part, core):
        if part == "a":
            return pl.ds(core * half, quarter)
        if part == "b":
            return pl.ds(core * half + quarter, quarter)
        return pl.ds(core * half, half)

    def l_copy(slot, unit, part, target, src=None, core=None):
        dst = lbuf.at[unit, :, l_rows(part, k if core is None else core), :]
        if src is not None:
            src = src.at[:, l_rows(part, 0), :]
        return remote(dst if src is None else src, dst, ls.at[slot], lr.at[slot], target)

    def l_send(slot, unit, part, target, src=None):
        c = l_copy(slot, unit, part, target, src)
        c.start()
        sends.append(c)
        return c

    def l_wait(slot, unit, part, core=None):
        l_copy(slot, unit, part, sibling, core=core).wait_recv()

    own_r, own_l = row, col // 2
    near = l_send(0, own_l, "", y_near, left)
    for i in range(PIECES):
        r_send(0, own_r, A, i, x_up, right)
        r_send(3, own_r, B, i, x_down, right)
    l_send(1, own_l, "a", z_up, left)
    l_send(4, own_l, "b", z_down, left)
    l_send(2, own_l, "b", z_up, left)
    l_send(3, own_l, "a", z_down, left)
    for i in range(PIECES):
        r_send(1, own_r, B, i, x_up, right)
        r_send(2, own_r, A, i, x_down, right)
    l_send(13, own_l, "", sibling, left)
    r_here.wait()
    for c in small:
        c.wait()
    e = jnp.broadcast_to(est[...], (8, width))
    psend[...] = jnp.zeros_like(psend)
    for g in range(groups):
        p = lax.dot_general(
            e, rbuf[own_r, g], (((1,), (1,)), ((), ())),
            precision=lax.Precision.HIGHEST, preferred_element_type=F32,
        )
        psend[g : g + 1, :] = p[0:1, :]
    for d in range(1, 16):
        c = remote(psend, pbuf.at[col], ps.at[d], pr.at[d], to_col((col + d) % 16))
        c.start()
        sends.append(c)
    offset = jnp.zeros((groups, n_obs), F32)
    ids = arc[...]
    for a in range(bias.shape[0]):
        offset = jnp.where(ids == a, bias[a], offset)
    pbuf[col] = psend[...]
    for d in range(1, 16):
        remote(psend, pbuf.at[(col + 16 - d) % 16], ps.at[d], pr.at[d], sibling).wait_recv()
    total = pbuf[0]
    for c in range(1, 16):
        total = total + pbuf[c]
    residual = obs[...] - total[:groups] - offset
    wbuf[row] = jnp.zeros_like(wbuf[0])
    wbuf[row, 0:groups, :] = 1.0 / (1.0 + residual * residual)
    for d in range(1, 8):
        c = remote(wbuf.at[row], wbuf.at[row], ws.at[d], wr.at[d], to_row((row + d) % 8))
        c.start()
        sends.append(c)

    def prepare(unit):
        def body(i, carry):
            cols = pl.ds(pl.multiple_of(i * TILE, TILE), TILE)
            for g in range(groups):
                t = lbuf[unit, g, :, cols].T * wbuf[unit, g : g + 1, :]
                hi = t.astype(BF16)
                lo = (t - hi.astype(F32)).astype(BF16)
                lt[unit, cols, g * n_obs : (g + 1) * n_obs] = hi
                lt[unit, cols, (groups + g) * n_obs : (groups + g + 1) * n_obs] = lo
            return carry

        lax.fori_loop(0, width // TILE, body, 0)

    depth = groups * n_obs

    def multiply_part(unit, i):
        cols = pl.ds(pl.multiple_of(i * TILE, TILE), TILE)
        t = rbuf[unit, :, :, cols].reshape(depth, TILE)
        hi = t.astype(BF16)
        lo = (t - hi.astype(F32)).astype(BF16)
        both = jnp.concatenate([hi, hi], axis=0)
        out[:, cols] += jnp.dot(lt[unit], both, preferred_element_type=F32) + jnp.dot(
            lt[unit, :, 0:depth], lo, preferred_element_type=F32
        )

    def multiply(*units):
        def body(i, carry):
            for unit in units:
                multiply_part(unit, i)
            return carry

        lax.fori_loop(0, PIECES, body, 0)

    def first(i):
        r_wait(0, unit_r(-1), A, i)
        if i not in ALONG_X:
            r_send(8, unit_r(-1), A, i, y_far)
        r_send(6, unit_r(-1), A, i, x_up)
        r_wait(3, unit_r(1), B, i)
        if i not in ALONG_X:
            r_send(9, unit_r(1), B, i, y_far)
        r_send(7, unit_r(1), B, i, x_down)

    def second(i):
        r_wait(4, unit_r(0, 1), A, i)
        if i in ALONG_X:
            r_send(8, unit_r(0, 1), A, i, x_up)
        r_send(10, unit_r(0, 1), A, i, x_down)
        r_wait(5, unit_r(0, 1), B, i)
        if i in ALONG_X:
            r_send(9, unit_r(0, 1), B, i, x_down)
        r_send(11, unit_r(0, 1), B, i, x_up)

    def third(i):
        r_wait(8, unit_r(-1, 1), A, i)
        r_send(12, unit_r(-1, 1), A, i, x_up)
        r_wait(9, unit_r(1, 1), B, i)
        r_send(13, unit_r(1, 1), B, i, x_down)

    near.wait_send()
    sends.remove(near)
    for i in range(PIECES):
        r_send(4, own_r, A, i, y_far, right)
        r_send(5, own_r, B, i, y_far, right)
    l_wait(1, unit_l(-1), "a")
    l_send(5, unit_l(-1), "a", z_up)
    l_wait(4, unit_l(1), "b")
    l_send(6, unit_l(1), "b", z_down)
    for i in range(PIECES):
        first(i)
    l_wait(0, unit_l(0, 1), "")
    l_send(7, unit_l(0, 1), "a", z_up)
    l_send(10, unit_l(0, 1), "b", z_down)
    l_send(8, unit_l(0, 1), "b", z_up)
    l_send(9, unit_l(0, 1), "a", z_down)
    l_send(14, unit_l(0, 1), "", sibling)
    for d in range(1, 8):
        u = (row + 8 - d) % 8
        remote(wbuf.at[row], wbuf.at[u], ws.at[d], wr.at[d], y_far).wait_recv()
    l_here.wait()
    l_wait(13, own_l, "", 1 - k)
    prepare(own_l)
    l_wait(2, unit_l(-1), "b")
    l_send(15, unit_l(-1), "", sibling)
    l_wait(3, unit_l(1), "a")
    l_send(16, unit_l(1), "", sibling)
    l_wait(14, unit_l(0, 1), "", 1 - k)
    prepare(unit_l(0, 1))
    second(0)
    l_wait(5, unit_l(2), "a")
    l_wait(6, unit_l(2), "b")
    l_send(17, unit_l(2), "", sibling)
    l_wait(15, unit_l(-1), "", 1 - k)
    prepare(unit_l(-1))
    l_wait(7, unit_l(-1, 1), "a")
    l_send(11, unit_l(-1, 1), "a", z_up)
    l_wait(10, unit_l(1, 1), "b")
    l_send(12, unit_l(1, 1), "b", z_down)
    second(1)
    l_wait(16, unit_l(1), "", 1 - k)
    prepare(unit_l(1))
    second(2)
    l_wait(17, unit_l(2), "", 1 - k)
    prepare(unit_l(2))
    l_wait(8, unit_l(-1, 1), "b")
    l_send(18, unit_l(-1, 1), "", sibling)
    l_wait(9, unit_l(1, 1), "a")
    l_send(19, unit_l(1, 1), "", sibling)
    second(3)
    l_wait(18, unit_l(-1, 1), "", 1 - k)
    prepare(unit_l(-1, 1))
    l_wait(11, unit_l(2, 1), "a")
    l_wait(12, unit_l(2, 1), "b")
    l_send(20, unit_l(2, 1), "", sibling)
    l_wait(19, unit_l(1, 1), "", 1 - k)
    prepare(unit_l(1, 1))
    s_here.wait()
    l_wait(20, unit_l(2, 1), "", 1 - k)
    prepare(unit_l(2, 1))
    multiply(own_r)
    third(0)
    r_all(1, unit_r(-1), B)
    multiply(unit_r(-1))
    third(1)
    r_all(2, unit_r(1), A)
    multiply(unit_r(1))
    multiply(unit_r(0, 1))
    third(2)
    r_all(6, unit_r(2), A)
    r_all(7, unit_r(2), B)
    multiply(unit_r(2))
    for i in range(PIECES):
        if i == PIECES - 1:
            third(i)
        r_wait(10, unit_r(1, 1), A, i)
        multiply_part(unit_r(1, 1), i)
        r_wait(11, unit_r(-1, 1), B, i)
        multiply_part(unit_r(-1, 1), i)
    for i in range(PIECES):
        r_wait(12, unit_r(2, 1), A, i)
        r_wait(13, unit_r(2, 1), B, i)
        multiply_part(unit_r(2, 1), i)
    for c in sends:
        c.wait_send()


def local(normal_slab, left_design, right_design, estimate, observed, arc_id, arc_bias):
    groups, n_obs, width = right_design.shape
    rows = left_design.shape[2]
    dma = pltpu.SemaphoreType.DMA
    return pl.pallas_call(
        kernel,
        name="gather_and_update",
        out_shape=pltpu.VMEM(normal_slab.shape, F32),
        in_specs=[pl.BlockSpec(memory_space=pltpu.HBM)] * 7,
        out_specs=pl.BlockSpec(memory_space=pltpu.VMEM),
        scratch_shapes=[
            pltpu.VMEM((8, groups, n_obs, width), F32),
            pltpu.VMEM((8, groups, n_obs, rows), F32),
            pltpu.VMEM((8, rows, 2 * groups * n_obs), BF16),
            pltpu.VMEM((8, n_obs), F32),
            pltpu.VMEM((16, 8, n_obs), F32),
            pltpu.VMEM((8, 8, n_obs), F32),
            pltpu.VMEM((1, width), F32),
            pltpu.VMEM((groups, n_obs), F32),
            pltpu.VMEM((groups, n_obs), jnp.int32),
            pltpu.SMEM(arc_bias.shape, F32),
            dma((14 * PIECES,)), dma((14 * PIECES,)), dma((21,)), dma((21,)),
            dma((16,)), dma((16,)), dma((8,)), dma((8,)), dma((7,)),
        ],
        compiler_params=pltpu.CompilerParams(
            collective_id=0, has_side_effects=True, vmem_limit_bytes=59 * 1024 * 1024
        ),
    )(estimate[None, :], observed, arc_id, arc_bias, normal_slab, left_design, right_design)


def solution(mesh):
    in_specs = (
        P("row", "col"),
        P(None, "col", "row"),
        P(None, "row", "col"),
        P("col"),
        P(None, "row"),
        P(None, "row"),
        P(),
    )
    return jax.shard_map(local, mesh=mesh, in_specs=in_specs, out_specs=P("row", "col"), check_vma=False)
```

```python
import functools

import jax
import jax.numpy as jnp
from jax import lax
from jax.experimental import pallas as pl
from jax.experimental.pallas import tpu as pltpu
from jax.sharding import PartitionSpec as P

MESH = pl.DeviceIdType.MESH
F32, BF16 = jnp.float32, jnp.bfloat16
NX, NZ = 4, 4
CHUNKS = ((0, 256), (256, 256), (512, 256), (768, 128), (896, 128))
OF_TILE = ((0,), (1,), (2,), (3, 4))
ALONG_X = (4,)
A, B = 0, 1
TILE = 256


def kernel(est_in, obs_in, arc_in, bias_in, slab, left, right, out, rbuf, lbuf, lt, psend, pbuf, wbuf,
           est, obs, arc, bias, rs, rr, ls, lr, ps, pr, ws, wr, cs):
    groups, n_obs, width = right.shape
    half, quarter = n_obs // 2, n_obs // 4
    row, col = lax.axis_index("row"), lax.axis_index("col")
    x, h = row // 2, row % 2
    z, l, k = col // 4, (col // 2) % 2, col % 2

    def unit_r(dx, flip=0):
        return ((x + dx) % NX) * 2 + (h + flip) % 2

    def unit_l(dz, flip=0):
        return ((z + dz) % NZ) * 2 + (l + flip) % 2

    def to_row(r):
        return (r, col)

    def to_col(c):
        return (row, c)

    x_up, x_down, y_far = to_row(unit_r(1)), to_row(unit_r(-1)), to_row(unit_r(0, 1))
    z_up, z_down = to_col(unit_l(1) * 2 + k), to_col(unit_l(-1) * 2 + k)
    y_near, sibling = to_col(unit_l(0, 1) * 2 + k), to_col((col // 2) * 2 + (1 - k))

    r_here = pltpu.make_async_copy(right, rbuf.at[row], cs.at[0])
    l_here = pltpu.make_async_copy(left, lbuf.at[col // 2, :, pl.ds(k * half, half), :], cs.at[1])
    s_here = pltpu.make_async_copy(slab, out, cs.at[2])
    small = [
        pltpu.make_async_copy(src, dst, cs.at[3 + i])
        for i, (src, dst) in enumerate([(est_in, est), (obs_in, obs), (arc_in, arc), (bias_in, bias)])
    ]
    for c in [r_here, *small, l_here, s_here]:
        c.start()

    barrier = pltpu.get_barrier_semaphore()
    for d in range(1, 16):
        pl.semaphore_signal(barrier, inc=1, device_id=to_col((col + d) % 16), device_id_type=MESH)
    for d in range(1, 8):
        pl.semaphore_signal(barrier, inc=1, device_id=to_row((row + d) % 8), device_id_type=MESH)
    r_here.wait()
    for c in small:
        c.wait()
    e = jnp.broadcast_to(est[...], (8, width))
    psend[...] = jnp.zeros_like(psend)
    for g in range(groups):
        p = lax.dot_general(
            e, rbuf[row, g], (((1,), (1,)), ((), ())),
            precision=lax.Precision.HIGHEST, preferred_element_type=F32,
        )
        psend[g : g + 1, :] = p[0:1, :]
    pl.semaphore_wait(barrier, 22)

    sends = []

    def remote(src, dst, s, r, target):
        return pltpu.make_async_remote_copy(
            src_ref=src, dst_ref=dst, send_sem=s, recv_sem=r, device_id=target, device_id_type=MESH
        )

    def r_copy(slot, unit, part, i, target, src=None):
        rows, cols = pl.ds(part * half, half), pl.ds(*CHUNKS[i])
        dst = rbuf.at[unit, :, rows, cols]
        s = slot * len(CHUNKS) + i
        return remote(dst if src is None else src.at[:, rows, cols], dst, rs.at[s], rr.at[s], target)

    def r_send(slot, unit, part, i, target, src=None):
        c = r_copy(slot, unit, part, i, target, src)
        c.start()
        sends.append(c)

    def r_wait(slot, unit, part, i):
        r_copy(slot, unit, part, i, y_far).wait_recv()

    def r_all(slot, unit, part):
        for i in range(len(CHUNKS)):
            r_wait(slot, unit, part, i)

    def l_rows(part, core):
        if part == "a":
            return pl.ds(core * half, quarter)
        if part == "b":
            return pl.ds(core * half + quarter, quarter)
        return pl.ds(core * half, half)

    def l_copy(slot, unit, part, target, src=None, core=None):
        dst = lbuf.at[unit, :, l_rows(part, k if core is None else core), :]
        if src is not None:
            src = src.at[:, l_rows(part, 0), :]
        return remote(dst if src is None else src, dst, ls.at[slot], lr.at[slot], target)

    def l_send(slot, unit, part, target, src=None):
        c = l_copy(slot, unit, part, target, src)
        c.start()
        sends.append(c)
        return c

    def l_wait(slot, unit, part, core=None):
        l_copy(slot, unit, part, sibling, core=core).wait_recv()

    own_r, own_l = row, col // 2
    for d in range(1, 16):
        c = remote(psend, pbuf.at[col], ps.at[d], pr.at[d], to_col((col + d) % 16))
        c.start()
        sends.append(c)
    near = l_send(0, own_l, "", y_near, left)
    for i in range(len(CHUNKS)):
        r_send(0, own_r, A, i, x_up, right)
        r_send(3, own_r, B, i, x_down, right)
    l_send(1, own_l, "a", z_up, left)
    l_send(4, own_l, "b", z_down, left)
    l_send(2, own_l, "b", z_up, left)
    l_send(3, own_l, "a", z_down, left)
    for i in range(len(CHUNKS)):
        r_send(1, own_r, B, i, x_up, right)
        r_send(2, own_r, A, i, x_down, right)
    l_send(13, own_l, "", sibling, left)
    def prepare(unit):
        def body(i, carry):
            cols = pl.ds(pl.multiple_of(i * TILE, TILE), TILE)
            for g in range(groups):
                t = lbuf[unit, g, :, cols].T * wbuf[unit, g : g + 1, :]
                hi = t.astype(BF16)
                lo = (t - hi.astype(F32)).astype(BF16)
                lt[unit, cols, g * n_obs : (g + 1) * n_obs] = hi
                lt[unit, cols, (groups + g) * n_obs : (groups + g + 1) * n_obs] = lo
            return carry

        lax.fori_loop(0, width // TILE, body, 0)

    depth = groups * n_obs

    def multiply_part(unit, i):
        cols = pl.ds(pl.multiple_of(i * TILE, TILE), TILE)
        t = rbuf[unit, :, :, cols].reshape(depth, TILE)
        hi = t.astype(BF16)
        lo = (t - hi.astype(F32)).astype(BF16)
        both = jnp.concatenate([hi, hi], axis=0)
        out[:, cols] += jnp.dot(lt[unit], both, preferred_element_type=F32) + jnp.dot(
            lt[unit, :, 0:depth], lo, preferred_element_type=F32
        )

    def multiply(*units):
        def body(i, carry):
            for unit in units:
                multiply_part(unit, i)
            return carry

        lax.fori_loop(0, width // TILE, body, 0)

    def first(i):
        r_wait(0, unit_r(-1), A, i)
        if i not in ALONG_X:
            r_send(8, unit_r(-1), A, i, y_far)
        r_send(6, unit_r(-1), A, i, x_up)
        r_wait(3, unit_r(1), B, i)
        if i not in ALONG_X:
            r_send(9, unit_r(1), B, i, y_far)
        r_send(7, unit_r(1), B, i, x_down)

    def second(i):
        r_wait(4, unit_r(0, 1), A, i)
        if i in ALONG_X:
            r_send(8, unit_r(0, 1), A, i, x_up)
        r_send(10, unit_r(0, 1), A, i, x_down)
        r_wait(5, unit_r(0, 1), B, i)
        if i in ALONG_X:
            r_send(9, unit_r(0, 1), B, i, x_down)
        r_send(11, unit_r(0, 1), B, i, x_up)

    def third(i):
        r_wait(8, unit_r(-1, 1), A, i)
        r_send(12, unit_r(-1, 1), A, i, x_up)
        r_wait(9, unit_r(1, 1), B, i)
        r_send(13, unit_r(1, 1), B, i, x_down)

    near.wait_send()
    sends[:] = [c for c in sends if c is not near]
    for i in range(len(CHUNKS)):
        r_send(4, own_r, A, i, y_far, right)
        r_send(5, own_r, B, i, y_far, right)
    l_wait(0, unit_l(0, 1), "")
    l_send(7, unit_l(0, 1), "a", z_up)
    l_send(10, unit_l(0, 1), "b", z_down)
    l_send(8, unit_l(0, 1), "b", z_up)
    l_send(9, unit_l(0, 1), "a", z_down)
    l_send(14, unit_l(0, 1), "", sibling)
    l_wait(1, unit_l(-1), "a")
    l_send(5, unit_l(-1), "a", z_up)
    l_wait(4, unit_l(1), "b")
    l_send(6, unit_l(1), "b", z_down)
    l_wait(2, unit_l(-1), "b")
    l_send(15, unit_l(-1), "", sibling)
    l_wait(3, unit_l(1), "a")
    l_send(16, unit_l(1), "", sibling)
    offset = jnp.zeros((groups, n_obs), F32)
    ids = arc[...]
    for a in range(bias.shape[0]):
        offset = jnp.where(ids == a, bias[a], offset)
    pbuf[col] = psend[...]
    for d in range(1, 16):
        remote(psend, pbuf.at[(col + 16 - d) % 16], ps.at[d], pr.at[d], sibling).wait_recv()
    total = pbuf[0]
    for c in range(1, 16):
        total = total + pbuf[c]
    residual = obs[...] - total[:groups] - offset
    wbuf[row] = jnp.zeros_like(wbuf[0])
    wbuf[row, 0:groups, :] = 1.0 / (1.0 + residual * residual)
    for d in range(1, 8):
        c = remote(wbuf.at[row], wbuf.at[row], ws.at[d], wr.at[d], to_row((row + d) % 8))
        c.start()
        sends.append(c)
    for i in range(len(CHUNKS)):
        first(i)
    for d in range(1, 8):
        u = (row + 8 - d) % 8
        remote(wbuf.at[row], wbuf.at[u], ws.at[d], wr.at[d], y_far).wait_recv()
    l_here.wait()
    l_wait(13, own_l, "", 1 - k)
    prepare(own_l)
    l_wait(14, unit_l(0, 1), "", 1 - k)
    prepare(unit_l(0, 1))
    l_wait(5, unit_l(2), "a")
    l_wait(6, unit_l(2), "b")
    l_send(17, unit_l(2), "", sibling)
    l_wait(15, unit_l(-1), "", 1 - k)
    prepare(unit_l(-1))
    l_wait(7, unit_l(-1, 1), "a")
    l_send(11, unit_l(-1, 1), "a", z_up)
    l_wait(10, unit_l(1, 1), "b")
    l_send(12, unit_l(1, 1), "b", z_down)
    l_wait(16, unit_l(1), "", 1 - k)
    prepare(unit_l(1))
    l_wait(8, unit_l(-1, 1), "b")
    l_send(18, unit_l(-1, 1), "", sibling)
    l_wait(9, unit_l(1, 1), "a")
    l_send(19, unit_l(1, 1), "", sibling)
    second(0)
    second(1)
    l_wait(17, unit_l(2), "", 1 - k)
    prepare(unit_l(2))
    l_wait(18, unit_l(-1, 1), "", 1 - k)
    prepare(unit_l(-1, 1))
    l_wait(19, unit_l(1, 1), "", 1 - k)
    prepare(unit_l(1, 1))
    second(2)
    s_here.wait()
    last = unit_l(2, 1)

    def early(unit):
        pl.when(unit != last)(lambda: multiply(unit))

    def late(unit):
        pl.when(unit == last)(lambda: multiply(unit))

    early(own_r)
    second(3)
    second(4)
    l_wait(11, unit_l(2, 1), "a")
    l_wait(12, unit_l(2, 1), "b")
    l_send(20, unit_l(2, 1), "", sibling)
    r_all(1, unit_r(-1), B)
    early(unit_r(-1))
    third(0)
    r_all(2, unit_r(1), A)
    early(unit_r(1))
    l_wait(20, unit_l(2, 1), "", 1 - k)
    prepare(last)
    late(own_r)
    late(unit_r(-1))
    late(unit_r(1))
    third(1)
    multiply(unit_r(0, 1))
    third(4)
    r_all(6, unit_r(2), A)
    r_all(7, unit_r(2), B)
    multiply(unit_r(2))
    for t, chunks in enumerate(OF_TILE):
        if t >= 2:
            third(t)
        for i in chunks:
            r_wait(10, unit_r(1, 1), A, i)
            r_wait(11, unit_r(-1, 1), B, i)
        multiply_part(unit_r(1, 1), t)
        multiply_part(unit_r(-1, 1), t)
    for t, chunks in enumerate(OF_TILE):
        for i in chunks:
            r_wait(12, unit_r(2, 1), A, i)
            r_wait(13, unit_r(2, 1), B, i)
        multiply_part(unit_r(2, 1), t)
    for c in sends:
        c.wait_send()


def local(normal_slab, left_design, right_design, estimate, observed, arc_id, arc_bias):
    groups, n_obs, width = right_design.shape
    rows = left_design.shape[2]
    dma = pltpu.SemaphoreType.DMA
    return pl.pallas_call(
        kernel,
        name="gather_and_update",
        out_shape=pltpu.VMEM(normal_slab.shape, F32),
        in_specs=[pl.BlockSpec(memory_space=pltpu.HBM)] * 7,
        out_specs=pl.BlockSpec(memory_space=pltpu.VMEM),
        scratch_shapes=[
            pltpu.VMEM((8, groups, n_obs, width), F32),
            pltpu.VMEM((8, groups, n_obs, rows), F32),
            pltpu.VMEM((8, rows, 2 * groups * n_obs), BF16),
            pltpu.VMEM((8, n_obs), F32),
            pltpu.VMEM((16, 8, n_obs), F32),
            pltpu.VMEM((8, 8, n_obs), F32),
            pltpu.VMEM((1, width), F32),
            pltpu.VMEM((groups, n_obs), F32),
            pltpu.VMEM((groups, n_obs), jnp.int32),
            pltpu.SMEM(arc_bias.shape, F32),
            dma((14 * len(CHUNKS),)), dma((14 * len(CHUNKS),)), dma((21,)), dma((21,)),
            dma((16,)), dma((16,)), dma((8,)), dma((8,)), dma((7,)),
        ],
        compiler_params=pltpu.CompilerParams(
            collective_id=0, has_side_effects=True, vmem_limit_bytes=59 * 1024 * 1024
        ),
    )(estimate[None, :], observed, arc_id, arc_bias, normal_slab, left_design, right_design)


def solution(mesh):
    in_specs = (
        P("row", "col"),
        P(None, "col", "row"),
        P(None, "row", "col"),
        P("col"),
        P(None, "row"),
        P(None, "row"),
        P(),
    )
    return jax.shard_map(local, mesh=mesh, in_specs=in_specs, out_specs=P("row", "col"), check_vma=False)
```

```python
import functools

import jax
import jax.numpy as jnp
from jax import lax
from jax.experimental import pallas as pl
from jax.experimental.pallas import tpu as pltpu
from jax.sharding import PartitionSpec as P

MESH = pl.DeviceIdType.MESH
F32, BF16 = jnp.float32, jnp.bfloat16
NX, NZ = 4, 4
CHUNKS = ((0, 256), (256, 256), (512, 256), (768, 128), (896, 128))
OF_TILE = ((0,), (1,), (2,), (3, 4))
ALONG_X = (4,)
A, B = 0, 1
TILE = 256


def kernel(est_in, obs_in, arc_in, bias_in, slab, left, right, out, rbuf, lbuf, lt, psend, pbuf, wbuf,
           est, obs, arc, bias, rs, rr, ls, lr, ps, pr, ws, wr, cs):
    groups, n_obs, width = right.shape
    half, quarter = n_obs // 2, n_obs // 4
    row, col = lax.axis_index("row"), lax.axis_index("col")
    x, h = row // 2, row % 2
    z, l, k = col // 4, (col // 2) % 2, col % 2

    def unit_r(dx, flip=0):
        return ((x + dx) % NX) * 2 + (h + flip) % 2

    def unit_l(dz, flip=0):
        return ((z + dz) % NZ) * 2 + (l + flip) % 2

    def to_row(r):
        return (r, col)

    def to_col(c):
        return (row, c)

    x_up, x_down, y_far = to_row(unit_r(1)), to_row(unit_r(-1)), to_row(unit_r(0, 1))
    z_up, z_down = to_col(unit_l(1) * 2 + k), to_col(unit_l(-1) * 2 + k)
    y_near, sibling = to_col(unit_l(0, 1) * 2 + k), to_col((col // 2) * 2 + (1 - k))

    r_here = pltpu.make_async_copy(right, rbuf.at[row], cs.at[0])
    l_here = pltpu.make_async_copy(left, lbuf.at[col // 2, :, pl.ds(k * half, half), :], cs.at[1])
    s_here = pltpu.make_async_copy(slab, out, cs.at[2])
    small = [
        pltpu.make_async_copy(src, dst, cs.at[3 + i])
        for i, (src, dst) in enumerate([(est_in, est), (obs_in, obs), (arc_in, arc), (bias_in, bias)])
    ]
    for c in [r_here, *small, l_here, s_here]:
        c.start()

    barrier = pltpu.get_barrier_semaphore()
    for d in range(1, 16):
        pl.semaphore_signal(barrier, inc=1, device_id=to_col((col + d) % 16), device_id_type=MESH)
    for d in range(1, 8):
        pl.semaphore_signal(barrier, inc=1, device_id=to_row((row + d) % 8), device_id_type=MESH)
    r_here.wait()
    for c in small:
        c.wait()
    e = jnp.broadcast_to(est[...], (8, width))
    psend[...] = jnp.zeros_like(psend)
    for g in range(groups):
        p = lax.dot_general(
            e, rbuf[row, g], (((1,), (1,)), ((), ())),
            precision=lax.Precision.HIGHEST, preferred_element_type=F32,
        )
        psend[g : g + 1, :] = p[0:1, :]
    pl.semaphore_wait(barrier, 22)

    sends = []

    def remote(src, dst, s, r, target):
        return pltpu.make_async_remote_copy(
            src_ref=src, dst_ref=dst, send_sem=s, recv_sem=r, device_id=target, device_id_type=MESH
        )

    def r_copy(slot, unit, part, i, target, src=None):
        rows, cols = pl.ds(part * half, half), pl.ds(*CHUNKS[i])
        dst = rbuf.at[unit, :, rows, cols]
        s = slot * len(CHUNKS) + i
        return remote(dst if src is None else src.at[:, rows, cols], dst, rs.at[s], rr.at[s], target)

    def r_send(slot, unit, part, i, target, src=None):
        c = r_copy(slot, unit, part, i, target, src)
        c.start()
        sends.append(c)

    def r_wait(slot, unit, part, i):
        r_copy(slot, unit, part, i, y_far).wait_recv()

    def r_all(slot, unit, part):
        for i in range(len(CHUNKS)):
            r_wait(slot, unit, part, i)

    def l_rows(part, core):
        if part == "a":
            return pl.ds(core * half, quarter)
        if part == "b":
            return pl.ds(core * half + quarter, quarter)
        return pl.ds(core * half, half)

    def l_copy(slot, unit, part, target, src=None, core=None):
        dst = lbuf.at[unit, :, l_rows(part, k if core is None else core), :]
        if src is not None:
            src = src.at[:, l_rows(part, 0), :]
        return remote(dst if src is None else src, dst, ls.at[slot], lr.at[slot], target)

    def l_send(slot, unit, part, target, src=None):
        c = l_copy(slot, unit, part, target, src)
        c.start()
        sends.append(c)
        return c

    def l_wait(slot, unit, part, core=None):
        l_copy(slot, unit, part, sibling, core=core).wait_recv()

    own_r, own_l = row, col // 2
    for d in range(1, 16):
        c = remote(psend, pbuf.at[col], ps.at[d], pr.at[d], to_col((col + d) % 16))
        c.start()
        sends.append(c)
    near = l_send(0, own_l, "", y_near, left)
    for i in range(len(CHUNKS)):
        r_send(0, own_r, A, i, x_up, right)
        r_send(3, own_r, B, i, x_down, right)
    l_send(1, own_l, "a", z_up, left)
    l_send(4, own_l, "b", z_down, left)
    l_send(2, own_l, "b", z_up, left)
    l_send(3, own_l, "a", z_down, left)
    l_send(13, own_l, "", sibling, left)
    def prepare(unit):
        def body(i, carry):
            cols = pl.ds(pl.multiple_of(i * TILE, TILE), TILE)
            for g in range(groups):
                t = lbuf[unit, g, :, cols].T * wbuf[unit, g : g + 1, :]
                hi = t.astype(BF16)
                lo = (t - hi.astype(F32)).astype(BF16)
                lt[unit, cols, g * n_obs : (g + 1) * n_obs] = hi
                lt[unit, cols, (groups + g) * n_obs : (groups + g + 1) * n_obs] = lo
            return carry

        lax.fori_loop(0, width // TILE, body, 0)

    depth = groups * n_obs

    def multiply_part(unit, i):
        cols = pl.ds(pl.multiple_of(i * TILE, TILE), TILE)
        t = rbuf[unit, :, :, cols].reshape(depth, TILE)
        hi = t.astype(BF16)
        lo = (t - hi.astype(F32)).astype(BF16)
        both = jnp.concatenate([hi, hi], axis=0)
        out[:, cols] += jnp.dot(lt[unit], both, preferred_element_type=F32) + jnp.dot(
            lt[unit, :, 0:depth], lo, preferred_element_type=F32
        )

    def multiply(*units):
        def body(i, carry):
            for unit in units:
                multiply_part(unit, i)
            return carry

        lax.fori_loop(0, width // TILE, body, 0)

    def first(i):
        r_wait(0, unit_r(-1), A, i)
        r_send(6, unit_r(-1), A, i, x_up)
        r_wait(3, unit_r(1), B, i)
        r_send(7, unit_r(1), B, i, x_down)

    def second(i):
        r_wait(4, unit_r(0, 1), A, i)
        if i in ALONG_X:
            r_send(8, unit_r(0, 1), A, i, x_up)
        r_send(10, unit_r(0, 1), A, i, x_down)
        r_wait(5, unit_r(0, 1), B, i)
        if i in ALONG_X:
            r_send(9, unit_r(0, 1), B, i, x_down)
        r_send(11, unit_r(0, 1), B, i, x_up)

    def cross(i):
        r_send(8, unit_r(-1), A, i, y_far)
        r_send(9, unit_r(1), B, i, y_far)

    def third(i):
        r_wait(8, unit_r(-1, 1), A, i)
        r_send(12, unit_r(-1, 1), A, i, x_up)
        r_wait(9, unit_r(1, 1), B, i)
        r_send(13, unit_r(1, 1), B, i, x_down)

    for i in range(2):
        first(i)
    for i in range(len(CHUNKS)):
        r_send(1, own_r, B, i, x_up, right)
        r_send(2, own_r, A, i, x_down, right)
    near.wait_send()
    sends[:] = [c for c in sends if c is not near]
    for i in range(2):
        r_send(4, own_r, A, i, y_far, right)
        r_send(5, own_r, B, i, y_far, right)
    l_wait(0, unit_l(0, 1), "")
    l_send(7, unit_l(0, 1), "a", z_up)
    l_send(10, unit_l(0, 1), "b", z_down)
    l_send(8, unit_l(0, 1), "b", z_up)
    l_send(9, unit_l(0, 1), "a", z_down)
    l_send(14, unit_l(0, 1), "", sibling)
    l_wait(1, unit_l(-1), "a")
    l_send(5, unit_l(-1), "a", z_up)
    l_wait(4, unit_l(1), "b")
    l_send(6, unit_l(1), "b", z_down)
    l_wait(2, unit_l(-1), "b")
    l_send(15, unit_l(-1), "", sibling)
    l_wait(3, unit_l(1), "a")
    l_send(16, unit_l(1), "", sibling)
    offset = jnp.zeros((groups, n_obs), F32)
    ids = arc[...]
    for a in range(bias.shape[0]):
        offset = jnp.where(ids == a, bias[a], offset)
    pbuf[col] = psend[...]
    for d in range(1, 16):
        remote(psend, pbuf.at[(col + 16 - d) % 16], ps.at[d], pr.at[d], sibling).wait_recv()
    total = pbuf[0]
    for c in range(1, 16):
        total = total + pbuf[c]
    residual = obs[...] - total[:groups] - offset
    wbuf[row] = jnp.zeros_like(wbuf[0])
    wbuf[row, 0:groups, :] = 1.0 / (1.0 + residual * residual)
    for d in range(1, 8):
        c = remote(wbuf.at[row], wbuf.at[row], ws.at[d], wr.at[d], to_row((row + d) % 8))
        c.start()
        sends.append(c)
    for i in range(2, len(CHUNKS)):
        first(i)
    for i in range(2, len(CHUNKS)):
        r_send(4, own_r, A, i, y_far, right)
        r_send(5, own_r, B, i, y_far, right)
    for d in range(1, 8):
        u = (row + 8 - d) % 8
        remote(wbuf.at[row], wbuf.at[u], ws.at[d], wr.at[d], y_far).wait_recv()
    l_here.wait()
    l_wait(13, own_l, "", 1 - k)
    prepare(own_l)
    l_wait(14, unit_l(0, 1), "", 1 - k)
    prepare(unit_l(0, 1))
    l_wait(5, unit_l(2), "a")
    l_wait(6, unit_l(2), "b")
    l_send(17, unit_l(2), "", sibling)
    l_wait(15, unit_l(-1), "", 1 - k)
    prepare(unit_l(-1))
    l_wait(7, unit_l(-1, 1), "a")
    l_send(11, unit_l(-1, 1), "a", z_up)
    l_wait(10, unit_l(1, 1), "b")
    l_send(12, unit_l(1, 1), "b", z_down)
    l_wait(16, unit_l(1), "", 1 - k)
    prepare(unit_l(1))
    l_wait(8, unit_l(-1, 1), "b")
    l_send(18, unit_l(-1, 1), "", sibling)
    l_wait(9, unit_l(1, 1), "a")
    l_send(19, unit_l(1, 1), "", sibling)
    second(0)
    second(1)
    cross(0)
    l_wait(17, unit_l(2), "", 1 - k)
    prepare(unit_l(2))
    l_wait(18, unit_l(-1, 1), "", 1 - k)
    prepare(unit_l(-1, 1))
    l_wait(19, unit_l(1, 1), "", 1 - k)
    prepare(unit_l(1, 1))
    second(2)
    cross(1)
    s_here.wait()
    last = unit_l(2, 1)

    def early(unit):
        pl.when(unit != last)(lambda: multiply(unit))

    def late(unit):
        pl.when(unit == last)(lambda: multiply(unit))

    early(own_r)
    second(3)
    cross(2)
    second(4)
    cross(3)
    l_wait(11, unit_l(2, 1), "a")
    l_wait(12, unit_l(2, 1), "b")
    l_send(20, unit_l(2, 1), "", sibling)
    r_all(1, unit_r(-1), B)
    early(unit_r(-1))
    r_all(2, unit_r(1), A)
    early(unit_r(1))
    early(unit_r(0, 1))
    third(0)
    r_all(6, unit_r(2), A)
    r_all(7, unit_r(2), B)
    early(unit_r(2))
    third(1)
    third(4)
    l_wait(20, unit_l(2, 1), "", 1 - k)
    prepare(last)
    late(own_r)
    late(unit_r(-1))
    late(unit_r(1))
    late(unit_r(0, 1))
    late(unit_r(2))
    for t, chunks in enumerate(OF_TILE):
        if t >= 2:
            third(t)
        for i in chunks:
            r_wait(10, unit_r(1, 1), A, i)
            r_wait(11, unit_r(-1, 1), B, i)
        multiply_part(unit_r(1, 1), t)
        multiply_part(unit_r(-1, 1), t)
    for t, chunks in enumerate(OF_TILE):
        for i in chunks:
            r_wait(12, unit_r(2, 1), A, i)
            r_wait(13, unit_r(2, 1), B, i)
        multiply_part(unit_r(2, 1), t)
    for c in sends:
        c.wait_send()


def local(normal_slab, left_design, right_design, estimate, observed, arc_id, arc_bias):
    groups, n_obs, width = right_design.shape
    rows = left_design.shape[2]
    dma = pltpu.SemaphoreType.DMA
    return pl.pallas_call(
        kernel,
        name="gather_and_update",
        out_shape=pltpu.VMEM(normal_slab.shape, F32),
        in_specs=[pl.BlockSpec(memory_space=pltpu.HBM)] * 7,
        out_specs=pl.BlockSpec(memory_space=pltpu.VMEM),
        scratch_shapes=[
            pltpu.VMEM((8, groups, n_obs, width), F32),
            pltpu.VMEM((8, groups, n_obs, rows), F32),
            pltpu.VMEM((8, rows, 2 * groups * n_obs), BF16),
            pltpu.VMEM((8, n_obs), F32),
            pltpu.VMEM((16, 8, n_obs), F32),
            pltpu.VMEM((8, 8, n_obs), F32),
            pltpu.VMEM((1, width), F32),
            pltpu.VMEM((groups, n_obs), F32),
            pltpu.VMEM((groups, n_obs), jnp.int32),
            pltpu.SMEM(arc_bias.shape, F32),
            dma((14 * len(CHUNKS),)), dma((14 * len(CHUNKS),)), dma((21,)), dma((21,)),
            dma((16,)), dma((16,)), dma((8,)), dma((8,)), dma((7,)),
        ],
        compiler_params=pltpu.CompilerParams(
            collective_id=0, has_side_effects=True, vmem_limit_bytes=59 * 1024 * 1024
        ),
    )(estimate[None, :], observed, arc_id, arc_bias, normal_slab, left_design, right_design)


def solution(mesh):
    in_specs = (
        P("row", "col"),
        P(None, "col", "row"),
        P(None, "row", "col"),
        P("col"),
        P(None, "row"),
        P(None, "row"),
        P(),
    )
    return jax.shard_map(local, mesh=mesh, in_specs=in_specs, out_specs=P("row", "col"), check_vma=False)
```

```python
import functools

import jax
import jax.numpy as jnp
from jax import lax
from jax.experimental import pallas as pl
from jax.experimental.pallas import tpu as pltpu
from jax.sharding import PartitionSpec as P

MESH = pl.DeviceIdType.MESH
F32, BF16 = jnp.float32, jnp.bfloat16
NX, NZ = 4, 4
CHUNKS = ((0, 256), (256, 256), (512, 256), (768, 128), (896, 128))
OF_TILE = ((0,), (1,), (2,), (3, 4))
ALONG_X = (4,)
A, B = 0, 1
TILE = 256


def kernel(est_in, obs_in, arc_in, bias_in, slab, left, right, out, rbuf, lbuf, lt, psend, pbuf, wbuf,
           est, obs, arc, bias, rs, rr, ls, lr, ps, pr, ws, wr, cs):
    groups, n_obs, width = right.shape
    half, quarter = n_obs // 2, n_obs // 4
    row, col = lax.axis_index("row"), lax.axis_index("col")
    x, h = row // 2, row % 2
    z, l, k = col // 4, (col // 2) % 2, col % 2

    def unit_r(dx, flip=0):
        return ((x + dx) % NX) * 2 + (h + flip) % 2

    def unit_l(dz, flip=0):
        return ((z + dz) % NZ) * 2 + (l + flip) % 2

    def to_row(r):
        return (r, col)

    def to_col(c):
        return (row, c)

    x_up, x_down, y_far = to_row(unit_r(1)), to_row(unit_r(-1)), to_row(unit_r(0, 1))
    z_up, z_down = to_col(unit_l(1) * 2 + k), to_col(unit_l(-1) * 2 + k)
    y_near, sibling = to_col(unit_l(0, 1) * 2 + k), to_col((col // 2) * 2 + (1 - k))

    r_here = pltpu.make_async_copy(right, rbuf.at[row], cs.at[0])
    l_here = pltpu.make_async_copy(left, lbuf.at[col // 2, :, pl.ds(k * half, half), :], cs.at[1])
    s_here = pltpu.make_async_copy(slab, out, cs.at[2])
    small = [
        pltpu.make_async_copy(src, dst, cs.at[3 + i])
        for i, (src, dst) in enumerate([(est_in, est), (obs_in, obs), (arc_in, arc), (bias_in, bias)])
    ]
    for c in [r_here, *small, l_here, s_here]:
        c.start()

    barrier = pltpu.get_barrier_semaphore()
    for d in range(1, 16):
        pl.semaphore_signal(barrier, inc=1, device_id=to_col((col + d) % 16), device_id_type=MESH)
    for d in range(1, 8):
        pl.semaphore_signal(barrier, inc=1, device_id=to_row((row + d) % 8), device_id_type=MESH)
    r_here.wait()
    for c in small:
        c.wait()
    e = jnp.broadcast_to(est[...], (8, width))
    psend[...] = jnp.zeros_like(psend)
    for g in range(groups):
        p = lax.dot_general(
            e, rbuf[row, g], (((1,), (1,)), ((), ())),
            precision=lax.Precision.HIGHEST, preferred_element_type=F32,
        )
        psend[g : g + 1, :] = p[0:1, :]
    pl.semaphore_wait(barrier, 22)

    sends = []

    def remote(src, dst, s, r, target):
        return pltpu.make_async_remote_copy(
            src_ref=src, dst_ref=dst, send_sem=s, recv_sem=r, device_id=target, device_id_type=MESH
        )

    def r_copy(slot, unit, part, i, target, src=None):
        rows, cols = pl.ds(part * half, half), pl.ds(*CHUNKS[i])
        dst = rbuf.at[unit, :, rows, cols]
        s = slot * len(CHUNKS) + i
        return remote(dst if src is None else src.at[:, rows, cols], dst, rs.at[s], rr.at[s], target)

    def r_send(slot, unit, part, i, target, src=None):
        c = r_copy(slot, unit, part, i, target, src)
        c.start()
        sends.append(c)

    def r_wait(slot, unit, part, i):
        r_copy(slot, unit, part, i, y_far).wait_recv()

    def r_all(slot, unit, part):
        for i in range(len(CHUNKS)):
            r_wait(slot, unit, part, i)

    def l_rows(part, core):
        if part == "a":
            return pl.ds(core * half, quarter)
        if part == "b":
            return pl.ds(core * half + quarter, quarter)
        return pl.ds(core * half, half)

    def l_copy(slot, unit, part, target, src=None, core=None):
        dst = lbuf.at[unit, :, l_rows(part, k if core is None else core), :]
        if src is not None:
            src = src.at[:, l_rows(part, 0), :]
        return remote(dst if src is None else src, dst, ls.at[slot], lr.at[slot], target)

    def l_send(slot, unit, part, target, src=None):
        c = l_copy(slot, unit, part, target, src)
        c.start()
        sends.append(c)
        return c

    def l_wait(slot, unit, part, core=None):
        l_copy(slot, unit, part, sibling, core=core).wait_recv()

    own_r, own_l = row, col // 2
    for d in range(1, 16):
        c = remote(psend, pbuf.at[col], ps.at[d], pr.at[d], to_col((col + d) % 16))
        c.start()
        sends.append(c)
    near = l_send(0, own_l, "", y_near, left)
    for i in range(len(CHUNKS)):
        r_send(0, own_r, A, i, x_up, right)
        r_send(3, own_r, B, i, x_down, right)
    l_send(1, own_l, "a", z_up, left)
    l_send(4, own_l, "b", z_down, left)
    l_send(2, own_l, "b", z_up, left)
    l_send(3, own_l, "a", z_down, left)
    l_send(13, own_l, "", sibling, left)
    def prepare(unit):
        def body(i, carry):
            cols = pl.ds(pl.multiple_of(i * TILE, TILE), TILE)
            for g in range(groups):
                t = lbuf[unit, g, :, cols].T * wbuf[unit, g : g + 1, :]
                hi = t.astype(BF16)
                lo = (t - hi.astype(F32)).astype(BF16)
                lt[unit, cols, g * n_obs : (g + 1) * n_obs] = hi
                lt[unit, cols, (groups + g) * n_obs : (groups + g + 1) * n_obs] = lo
            return carry

        lax.fori_loop(0, width // TILE, body, 0)

    depth = groups * n_obs

    def multiply_part(unit, i):
        cols = pl.ds(pl.multiple_of(i * TILE, TILE), TILE)
        t = rbuf[unit, :, :, cols].reshape(depth, TILE)
        hi = t.astype(BF16)
        lo = (t - hi.astype(F32)).astype(BF16)
        both = jnp.concatenate([hi, hi], axis=0)
        out[:, cols] += jnp.dot(lt[unit], both, preferred_element_type=F32) + jnp.dot(
            lt[unit, :, 0:depth], lo, preferred_element_type=F32
        )

    def multiply(*units):
        def body(i, carry):
            for unit in units:
                multiply_part(unit, i)
            return carry

        lax.fori_loop(0, width // TILE, body, 0)

    def first(i):
        r_wait(0, unit_r(-1), A, i)
        r_send(6, unit_r(-1), A, i, x_up)
        r_wait(3, unit_r(1), B, i)
        r_send(7, unit_r(1), B, i, x_down)

    def second(i):
        r_wait(4, unit_r(0, 1), A, i)
        if i in ALONG_X:
            r_send(8, unit_r(0, 1), A, i, x_up)
        r_send(10, unit_r(0, 1), A, i, x_down)
        r_wait(5, unit_r(0, 1), B, i)
        if i in ALONG_X:
            r_send(9, unit_r(0, 1), B, i, x_down)
        r_send(11, unit_r(0, 1), B, i, x_up)

    def cross(i):
        r_send(8, unit_r(-1), A, i, y_far)
        r_send(9, unit_r(1), B, i, y_far)

    def third(i):
        r_wait(8, unit_r(-1, 1), A, i)
        r_send(12, unit_r(-1, 1), A, i, x_up)
        r_wait(9, unit_r(1, 1), B, i)
        r_send(13, unit_r(1, 1), B, i, x_down)

    for i in range(2):
        first(i)
    for i in range(len(CHUNKS)):
        r_send(1, own_r, B, i, x_up, right)
        r_send(2, own_r, A, i, x_down, right)
    near.wait_send()
    sends[:] = [c for c in sends if c is not near]
    for i in range(2):
        r_send(4, own_r, A, i, y_far, right)
        r_send(5, own_r, B, i, y_far, right)
    l_wait(0, unit_l(0, 1), "")
    l_send(7, unit_l(0, 1), "a", z_up)
    l_send(10, unit_l(0, 1), "b", z_down)
    l_send(8, unit_l(0, 1), "b", z_up)
    l_send(9, unit_l(0, 1), "a", z_down)
    l_send(14, unit_l(0, 1), "", sibling)
    l_wait(1, unit_l(-1), "a")
    l_send(5, unit_l(-1), "a", z_up)
    l_wait(4, unit_l(1), "b")
    l_send(6, unit_l(1), "b", z_down)
    l_wait(2, unit_l(-1), "b")
    l_send(15, unit_l(-1), "", sibling)
    l_wait(3, unit_l(1), "a")
    l_send(16, unit_l(1), "", sibling)
    offset = jnp.zeros((groups, n_obs), F32)
    ids = arc[...]
    for a in range(bias.shape[0]):
        offset = jnp.where(ids == a, bias[a], offset)
    pbuf[col] = psend[...]
    for d in range(1, 16):
        remote(psend, pbuf.at[(col + 16 - d) % 16], ps.at[d], pr.at[d], sibling).wait_recv()
    total = pbuf[0]
    for c in range(1, 16):
        total = total + pbuf[c]
    residual = obs[...] - total[:groups] - offset
    wbuf[row] = jnp.zeros_like(wbuf[0])
    wbuf[row, 0:groups, :] = 1.0 / (1.0 + residual * residual)
    for d in range(1, 8):
        c = remote(wbuf.at[row], wbuf.at[row], ws.at[d], wr.at[d], to_row((row + d) % 8))
        c.start()
        sends.append(c)
    for i in range(2, len(CHUNKS)):
        first(i)
    for i in range(2, len(CHUNKS)):
        r_send(4, own_r, A, i, y_far, right)
        r_send(5, own_r, B, i, y_far, right)
    for d in range(1, 8):
        u = (row + 8 - d) % 8
        remote(wbuf.at[row], wbuf.at[u], ws.at[d], wr.at[d], y_far).wait_recv()
    l_here.wait()
    l_wait(13, own_l, "", 1 - k)
    prepare(own_l)
    l_wait(14, unit_l(0, 1), "", 1 - k)
    prepare(unit_l(0, 1))
    l_wait(5, unit_l(2), "a")
    l_wait(6, unit_l(2), "b")
    l_send(17, unit_l(2), "", sibling)
    l_wait(15, unit_l(-1), "", 1 - k)
    prepare(unit_l(-1))
    l_wait(7, unit_l(-1, 1), "a")
    l_send(11, unit_l(-1, 1), "a", z_up)
    l_wait(10, unit_l(1, 1), "b")
    l_send(12, unit_l(1, 1), "b", z_down)
    l_wait(16, unit_l(1), "", 1 - k)
    prepare(unit_l(1))
    l_wait(8, unit_l(-1, 1), "b")
    l_send(18, unit_l(-1, 1), "", sibling)
    l_wait(9, unit_l(1, 1), "a")
    l_send(19, unit_l(1, 1), "", sibling)
    second(0)
    second(1)
    cross(0)
    l_wait(17, unit_l(2), "", 1 - k)
    prepare(unit_l(2))
    l_wait(18, unit_l(-1, 1), "", 1 - k)
    prepare(unit_l(-1, 1))
    l_wait(19, unit_l(1, 1), "", 1 - k)
    prepare(unit_l(1, 1))
    s_here.wait()
    last = unit_l(2, 1)

    def early(unit):
        pl.when(unit != last)(lambda: multiply(unit))

    def late(unit):
        pl.when(unit == last)(lambda: multiply(unit))

    early(own_r)
    second(2)
    cross(1)
    r_all(1, unit_r(-1), B)
    early(unit_r(-1))
    second(3)
    cross(2)
    second(4)
    cross(3)
    r_all(2, unit_r(1), A)
    early(unit_r(1))
    l_wait(11, unit_l(2, 1), "a")
    l_wait(12, unit_l(2, 1), "b")
    l_send(20, unit_l(2, 1), "", sibling)
    early(unit_r(0, 1))
    third(0)
    r_all(6, unit_r(2), A)
    r_all(7, unit_r(2), B)
    early(unit_r(2))
    l_wait(20, unit_l(2, 1), "", 1 - k)
    prepare(last)
    late(own_r)
    late(unit_r(-1))
    late(unit_r(1))
    late(unit_r(0, 1))
    late(unit_r(2))
    third(1)
    third(4)
    def pair(t):
        for i in OF_TILE[t]:
            r_wait(10, unit_r(1, 1), A, i)
            r_wait(11, unit_r(-1, 1), B, i)
        multiply_part(unit_r(1, 1), t)
        multiply_part(unit_r(-1, 1), t)

    def final(t):
        for i in OF_TILE[t]:
            r_wait(12, unit_r(2, 1), A, i)
            r_wait(13, unit_r(2, 1), B, i)
        multiply_part(unit_r(2, 1), t)

    pair(0)
    pair(1)
    final(0)
    third(2)
    pair(2)
    final(1)
    third(3)
    pair(3)
    final(2)
    final(3)
    for c in sends:
        c.wait_send()


def local(normal_slab, left_design, right_design, estimate, observed, arc_id, arc_bias):
    groups, n_obs, width = right_design.shape
    rows = left_design.shape[2]
    dma = pltpu.SemaphoreType.DMA
    return pl.pallas_call(
        kernel,
        name="gather_and_update",
        out_shape=pltpu.VMEM(normal_slab.shape, F32),
        in_specs=[pl.BlockSpec(memory_space=pltpu.HBM)] * 7,
        out_specs=pl.BlockSpec(memory_space=pltpu.VMEM),
        scratch_shapes=[
            pltpu.VMEM((8, groups, n_obs, width), F32),
            pltpu.VMEM((8, groups, n_obs, rows), F32),
            pltpu.VMEM((8, rows, 2 * groups * n_obs), BF16),
            pltpu.VMEM((8, n_obs), F32),
            pltpu.VMEM((16, 8, n_obs), F32),
            pltpu.VMEM((8, 8, n_obs), F32),
            pltpu.VMEM((1, width), F32),
            pltpu.VMEM((groups, n_obs), F32),
            pltpu.VMEM((groups, n_obs), jnp.int32),
            pltpu.SMEM(arc_bias.shape, F32),
            dma((14 * len(CHUNKS),)), dma((14 * len(CHUNKS),)), dma((21,)), dma((21,)),
            dma((16,)), dma((16,)), dma((8,)), dma((8,)), dma((7,)),
        ],
        compiler_params=pltpu.CompilerParams(
            collective_id=0, has_side_effects=True, vmem_limit_bytes=59 * 1024 * 1024
        ),
    )(estimate[None, :], observed, arc_id, arc_bias, normal_slab, left_design, right_design)


def solution(mesh):
    in_specs = (
        P("row", "col"),
        P(None, "col", "row"),
        P(None, "row", "col"),
        P("col"),
        P(None, "row"),
        P(None, "row"),
        P(),
    )
    return jax.shard_map(local, mesh=mesh, in_specs=in_specs, out_specs=P("row", "col"), check_vma=False)
```
